32 devices in a mesh: dp: 8 (over y, x, core), tensor: 4 (over z).
Axes of the slice: x: 2, y: 2, z: 4, core: 2. Of those that a mesh axis runs over, the one named last changes fastest.
Arguments:
- tokens: bfloat16 [24, 256, 768], P('dp', 'tensor'), may hold values from -32 to 32
- counts: int32 [24, 4], P('dp'), may hold values from 1 to 64, 197 in all within a row
- w_qkv: bfloat16 [3, 768, 768], P(None, 'dp', 'tensor'), may hold values from -4 to 4
- b_qv: bfloat16 [2, 12, 64], P(None, 'tensor', 'dp'), may hold values from -3 to 3
- w_out: bfloat16 [768, 768], P('tensor', 'dp'), may hold values from -0.875 to 0.875
- w_fc1: bfloat16 [768, 3072], P('dp', 'tensor'), may hold values from -0.21875 to 0.21875
- b_fc1: bfloat16 [48, 64], P('tensor', 'dp'), may hold values from -3 to 3
- w_fc2: bfloat16 [3072, 768], P('tensor', 'dp'), may hold values from -0.109375 to 0.109375
- ln_gain: bfloat16 [2, 768], P(None, 'dp'), may hold values from 0.25 to 1.75
- vec_bias: bfloat16 [4, 768], P(None, 'dp'), may hold values from -3 to 3
- cotangent: bfloat16 [24, 256, 768], P('dp', 'tensor'), may hold values from -6 to 6
Outputs:
- out: bfloat16 [24, 256, 768], P('dp', 'tensor')
- grad_tokens: bfloat16 [24, 256, 768], P('dp', 'tensor')
- grad_qkv: float32 [3, 768, 768], P(None, 'dp', 'tensor')
- grad_out: float32 [768, 768], P('tensor', 'dp')
- grad_fc1: float32 [768, 3072], P('dp', 'tensor')
- grad_fc2: float32 [3072, 768], P('tensor', 'dp')
- grad_bqv: float32 [2, 12, 64], P(None, 'tensor', 'dp')
- grad_bfc1: float32 [48, 64], P('tensor', 'dp')
- grad_gain: float32 [2, 768], P(None, ('dp', 'tensor'))
- grad_vbias: float32 [4, 768], P(None, ('dp', 'tensor'))
The draws below stay inside these ranges and needn't reach their ends.
Inputs may be any that keep to these rules, and one draw needn't show every extreme that they name: `counts`: row i lists how many of image i's 197 tokens each index of tensor holds, in token order; every row sums to 197 and its largest entry is 64.
All inputs are finite; a program needn't handle non-finite values.
Results may differ from the reference program's by a relative error of at most 0.011.
Values may be sent and summed in bfloat16 or wider, within the bound.
A program may use at most 128 MiB of HBM per device.

```python
import math
import jax
import jax.numpy as jnp
import numpy as np
from jax import lax

D = 768
H = 12
DH = 64
FF = 3072
SEQ = 197
CAP = 64
IMAGES = 24
TPARTS = 4
SLOTS = 256


def draw_tokens(key, part):
    base_key, row_key = jax.random.split(key, 2)
    row_scale = jnp.exp(jax.random.uniform(row_key, (IMAGES, SLOTS, 1), jnp.float32, math.log(0.3), math.log(3.0)))
    base_draw = jnp.clip(jax.random.normal(base_key, (IMAGES, SLOTS, D), jnp.float32), -6.0, 6.0)
    return (base_draw * row_scale).astype(jnp.bfloat16)


def draw_w_qkv(key, part):
    drawn_key = jax.random.fold_in(key, 0)
    drawn_draw = jnp.clip(jax.random.normal(drawn_key, (3, D, D), jnp.float32), -6.0, 6.0) / math.sqrt(D)
    return drawn_draw.astype(jnp.bfloat16)


def with_spikes(values, stream_key, source, target, shards_of, factor):
    def block_of(dim):
        return (jnp.arange(values.shape[dim]) // (values.shape[dim] // shards_of)).reshape((-1,) + (1,) * (values.ndim - 1 - dim))

    near = jax.random.permutation(stream_key, shards_of)[block_of(target)]
    second = (block_of(target) + shards_of // 2) % shards_of
    return jnp.where((block_of(source) == near) | (block_of(source) == second), factor * values, values)


def steps_of(own_key, extent, cuts, smallest, largest):
    def one(dim, shards_of):
        steps = jax.random.uniform(jax.random.fold_in(jax.random.fold_in(own_key, 6), dim), (shards_of,), jnp.float32, smallest / len(cuts), largest / len(cuts))
        return jnp.repeat(jnp.exp(steps), extent[dim] // shards_of).reshape((-1,) + (1,) * (len(extent) - dim - 1))

    loudness = one(*cuts[0])
    for cut in cuts[1:]:
        loudness = loudness * one(*cut)
    return loudness


def split_up(count, total, limit, lean):
    weights = [(1 << 20) // math.isqrt(grade ** lean) + 1 for grade in range(2, count + 1)]
    surplus, given = total - limit - (count - 1), [1] * (count - 1)
    while surplus > 0:
        movable = [i for i in range(count - 1) if given[i] < limit]
        mass, budget = sum([weights[i] for i in movable]), surplus
        for i in movable:
            extra = min(limit - given[i], max(1, budget * weights[i] // mass), surplus)
            given[i] = given[i] + extra
            surplus = surplus - extra
    return np.array([limit] + given)


def ragged(key, amount, total, limit, slope):
    if amount == 2:
        one = jax.random.randint(key, (), max(1, total - limit), min(limit, total - 1) + 1)
        return jnp.stack([one, total - one])
    lengths = jnp.asarray(split_up(amount, total, limit, slope), jnp.int32)
    pairs = (amount - 1) // 2
    source_of, sink = lengths[1:1 + 2 * pairs:2], lengths[2:2 + 2 * pairs:2]
    room = jnp.minimum(source_of - 1, limit - sink)
    shifted = jax.random.randint(jax.random.fold_in(key, 1), (pairs,), 0, 1 << 20) % (room + 1)
    lengths = lengths.at[1:1 + 2 * pairs:2].set(source_of - shifted).at[2:2 + 2 * pairs:2].set(sink + shifted)
    return lengths[jax.random.permutation(jax.random.fold_in(key, 2), amount)]


def noise(key, dims, width, limit, shards=(), kind=jnp.bfloat16):
    entries = jax.random.normal(key, dims, jnp.float32) * width
    if len(shards) > 0:
        entries = steps_of(key, dims, shards, -0.22, 0.18) * entries
    return jnp.clip(entries, min=-limit, max=limit).astype(kind)


def bell_draw_with(rng, extent, deviation, most, cuts, heavy, kind=jnp.bfloat16):
    entries = deviation * jax.random.normal(rng, extent, jnp.float32)
    if cuts:
        entries = entries * steps_of(rng, extent, cuts, -0.22, 0.18)
    return jnp.clip(with_spikes(entries, jax.random.fold_in(rng, 3), *heavy), -most, most).astype(kind)


def setup_inputs(seed: int = 0) -> dict:
    splits = jax.random.split(jax.random.key(seed), 12)
    return {
        "tokens": draw_tokens(jax.random.fold_in(splits[11], 71), 0),
        "counts": jax.vmap(lambda own: ragged(own, TPARTS, SEQ, CAP, 2))(jax.random.split(splits[1], IMAGES)).reshape((IMAGES, TPARTS)).astype(jnp.int32),
        "w_qkv": draw_w_qkv(jax.random.fold_in(splits[11], 71), 0),
        "b_qv": noise(splits[3], (2, H, DH), 0.5, 3.0, ((1, 4), (2, 8))),
        "w_out": noise(splits[4], (D, D), (D // 16) ** -0.5, 0.875, ((0, 4), (1, 8))),
        "w_fc1": noise(splits[5], (D, FF), D ** -0.5, 0.21875, ((0, 8), (1, 4))),
        "b_fc1": noise(splits[6], (FF // DH, DH), 0.5, 3.0, ((0, 4), (1, 8))),
        "w_fc2": noise(splits[7], (FF, D), FF ** -0.5, 0.109375, ((0, 4), (1, 8))),
        "ln_gain": jnp.clip(1.0 + 0.15 * jax.random.normal(splits[8], (2, D), jnp.float32), 0.25, 1.75).astype(jnp.bfloat16),
        "vec_bias": noise(splits[9], (4, D), 0.5, 3.0, ((1, 8),)),
        "cotangent": bell_draw_with(splits[10], (IMAGES, SLOTS, D), 1.0, 6.0, ((0, 8), (1, 4)), (0, 2, 8, 2.0)),
    }


LN_EPS = 1e-06
HALF_ROOT = 0.7071067811865476
INV_ROOT_TAU = 0.3989422804014327

def norm_statistics(values):
    centered = values - lax.optimization_barrier(jnp.mean(values, axis=-1, keepdims=True))
    variance = lax.optimization_barrier(jnp.mean(centered * centered, axis=-1, keepdims=True))
    inverse_deviation = lax.rsqrt(variance + LN_EPS)
    return (centered * inverse_deviation, inverse_deviation)

def norm_backward(incoming_gradient, gain_row_vector, centered_unit, inverse_deviation):
    scaled_rows = incoming_gradient * gain_row_vector
    return inverse_deviation * (scaled_rows - lax.optimization_barrier(jnp.mean(scaled_rows, axis=-1, keepdims=True)) - centered_unit * lax.optimization_barrier(jnp.mean(scaled_rows * centered_unit, axis=-1, keepdims=True)))

def gelu_parts(pre_act):
    normal_cdf = 0.5 * (1.0 + lax.erf(pre_act * HALF_ROOT))
    density = jnp.exp(-0.5 * pre_act * pre_act) * INV_ROOT_TAU
    return (normal_cdf, density)

def token_index(counts, capacity):
    starts = jnp.cumsum(counts, axis=1) - counts
    position = jnp.arange(SEQ, dtype=jnp.int32)
    owner_index = lax.optimization_barrier(jnp.sum((position[None, :, None] >= starts[:, None, 1:]).astype(jnp.int32), axis=2)).astype(jnp.int32)
    first_token = jnp.take_along_axis(starts, owner_index, axis=1)
    return ((owner_index * capacity + position[None, :] - first_token).astype(jnp.int32), owner_index)

def slot_index(counts, capacity):
    part_count = counts.shape[1]
    starts = jnp.cumsum(counts, axis=1) - counts
    slot_ids = jnp.arange(part_count * capacity, dtype=jnp.int32)
    holder = slot_ids // capacity
    offset = slot_ids % capacity
    live_slot = offset[None, :] < jnp.take(counts, holder, axis=1)
    target = jnp.where(live_slot, jnp.take(starts, holder, axis=1) + offset[None, :], 0).astype(jnp.int32)
    return (target, live_slot)

def reference(tokens, counts, w_qkv, b_qv, w_out, w_fc1, b_fc1, w_fc2, ln_gain, vec_bias, cotangent):
    gather_index, owner_index = token_index(counts, CAP)
    slot_target, slot_live = slot_index(counts, CAP)
    ordered = jnp.take_along_axis(tokens, gather_index[:, :, None], axis=1)
    ordered_cot = jnp.take_along_axis(cotangent, gather_index[:, :, None], axis=1)
    gains_wide = ln_gain.astype(jnp.float32)
    biases_wide = vec_bias.astype(jnp.float32)
    first_gain = gains_wide[0]
    second_gain = gains_wide[1]
    first_shift = biases_wide[0]
    out_bias = biases_wide[1]
    second_shift = biases_wide[2]
    fc2_bias = biases_wide[3]
    bias_q = b_qv[0].astype(jnp.float32).reshape(D)
    bias_v = b_qv[1].astype(jnp.float32).reshape(D)
    hidden_bias = b_fc1.astype(jnp.float32).reshape(FF)
    score_scale = 1.0 / math.sqrt(DH)

    def one_image(totals, inputs):
        image_rows, image_cot = inputs
        token_float = image_rows.astype(jnp.float32)
        first_centered_unit, first_inverse_deviation = norm_statistics(token_float)
        first_normalized_rows = (first_centered_unit * first_gain + first_shift).astype(jnp.bfloat16)
        queries = (jnp.dot(first_normalized_rows, w_qkv[0], preferred_element_type=jnp.float32) + bias_q).astype(jnp.bfloat16)
        keys_all = jnp.dot(first_normalized_rows, w_qkv[1], preferred_element_type=jnp.float32).astype(jnp.bfloat16)
        values_all = (jnp.dot(first_normalized_rows, w_qkv[2], preferred_element_type=jnp.float32) + bias_v).astype(jnp.bfloat16)
        q_heads = queries.astype(jnp.float32).reshape(SEQ, H, DH)
        k_heads = keys_all.astype(jnp.float32).reshape(SEQ, H, DH)
        v_heads = values_all.astype(jnp.float32).reshape(SEQ, H, DH)
        scores = jnp.einsum('qhd,khd->hqk', q_heads, k_heads) * score_scale
        row_top = lax.optimization_barrier(jnp.max(scores, axis=2, keepdims=True))
        log_total = row_top + jnp.log(lax.optimization_barrier(jnp.sum(jnp.exp(scores - row_top), axis=2, keepdims=True)))
        probs = jnp.exp(scores - log_total)
        probs_bf = probs.astype(jnp.bfloat16)
        attended = jnp.einsum('hqk,khd->qhd', probs_bf.astype(jnp.float32), v_heads).astype(jnp.bfloat16).reshape(SEQ, D)
        residual_stream = token_float + jnp.dot(attended, w_out, preferred_element_type=jnp.float32) + out_bias
        second_centered_unit, second_inverse_deviation = norm_statistics(residual_stream)
        second_normalized_rows = (second_centered_unit * second_gain + second_shift).astype(jnp.bfloat16)
        hidden_pre = jnp.dot(second_normalized_rows, w_fc1, preferred_element_type=jnp.float32) + hidden_bias
        normal_cdf, density = gelu_parts(hidden_pre)
        hidden = (hidden_pre * normal_cdf).astype(jnp.bfloat16)
        result = (residual_stream + jnp.dot(hidden, w_fc2, preferred_element_type=jnp.float32) + fc2_bias).astype(jnp.bfloat16)
        cotangent_float = image_cot.astype(jnp.float32)
        d_fc2 = jnp.dot(hidden.T, image_cot, preferred_element_type=jnp.float32)
        d_hidden = jnp.dot(image_cot, w_fc2.T, preferred_element_type=jnp.float32) * (normal_cdf + hidden_pre * density)
        d_hidden_bf = d_hidden.astype(jnp.bfloat16)
        d_fc1 = jnp.dot(second_normalized_rows.T, d_hidden_bf, preferred_element_type=jnp.float32)
        second_normalized_gradient = jnp.dot(d_hidden_bf, w_fc1.T, preferred_element_type=jnp.float32)
        residual_gradient = cotangent_float + norm_backward(second_normalized_gradient, second_gain, second_centered_unit, second_inverse_deviation)
        d_resid_bf = residual_gradient.astype(jnp.bfloat16)
        d_out = jnp.dot(attended.T, d_resid_bf, preferred_element_type=jnp.float32)
        d_attended = jnp.dot(d_resid_bf, w_out.T, preferred_element_type=jnp.float32).astype(jnp.bfloat16)
        da_heads = d_attended.astype(jnp.float32).reshape(SEQ, H, DH)
        d_values = jnp.einsum('hqk,qhd->khd', probs_bf.astype(jnp.float32), da_heads)
        d_probs = jnp.einsum('qhd,khd->hqk', da_heads, v_heads)
        row_delta = lax.optimization_barrier(jnp.sum(probs * d_probs, axis=2, keepdims=True))
        d_scores = (probs * (d_probs - row_delta) * score_scale).astype(jnp.bfloat16).astype(jnp.float32)
        d_queries = jnp.einsum('hqk,khd->qhd', d_scores, k_heads)
        d_keys = jnp.einsum('hqk,qhd->khd', d_scores, q_heads)
        stacked = jnp.stack([d_queries, d_keys, d_values]).reshape(3, SEQ, D).astype(jnp.bfloat16)
        d_qkv = jnp.stack([jnp.dot(first_normalized_rows.T, stacked[which], preferred_element_type=jnp.float32) for which in range(3)])
        first_normalized_gradient = jnp.dot(stacked[0], w_qkv[0].T, preferred_element_type=jnp.float32)
        first_normalized_gradient = first_normalized_gradient + jnp.dot(stacked[1], w_qkv[1].T, preferred_element_type=jnp.float32)
        first_normalized_gradient = first_normalized_gradient + jnp.dot(stacked[2], w_qkv[2].T, preferred_element_type=jnp.float32)
        token_gradient = (residual_gradient + norm_backward(first_normalized_gradient, first_gain, first_centered_unit, first_inverse_deviation)).astype(jnp.bfloat16)
        g_bqv = jnp.stack([lax.optimization_barrier(jnp.sum(d_queries, axis=0)), lax.optimization_barrier(jnp.sum(d_values, axis=0))]).reshape(2, D)
        g_bfc1 = lax.optimization_barrier(jnp.sum(d_hidden, axis=0))
        gain_gradient = jnp.stack([lax.optimization_barrier(jnp.sum(first_normalized_gradient * first_centered_unit, axis=0)), lax.optimization_barrier(jnp.sum(second_normalized_gradient * second_centered_unit, axis=0))])
        g_vbias = jnp.stack([lax.optimization_barrier(jnp.sum(first_normalized_gradient, axis=0)), lax.optimization_barrier(jnp.sum(residual_gradient, axis=0)), lax.optimization_barrier(jnp.sum(second_normalized_gradient, axis=0)), lax.optimization_barrier(jnp.sum(cotangent_float, axis=0))])
        terms = (d_qkv, d_out, d_fc1, d_fc2, g_bqv, g_bfc1, gain_gradient, g_vbias)
        return (tuple((left + right for left, right in zip(totals, terms))), (result, token_gradient))
    start_totals = (jnp.zeros((3, D, D), jnp.float32), jnp.zeros((D, D), jnp.float32), jnp.zeros((D, FF), jnp.float32), jnp.zeros((FF, D), jnp.float32), jnp.zeros((2, D), jnp.float32), jnp.zeros((FF,), jnp.float32), jnp.zeros((2, D), jnp.float32), jnp.zeros((4, D), jnp.float32))
    totals, (out_rows, grad_rows) = lax.scan(one_image, start_totals, (ordered, ordered_cot))
    live_cols = slot_live[:, :, None]
    out_slots = jnp.where(live_cols, jnp.take_along_axis(out_rows, slot_target[:, :, None], axis=1), jnp.zeros((), jnp.bfloat16)).astype(jnp.bfloat16)
    grad_slots = jnp.where(live_cols, jnp.take_along_axis(grad_rows, slot_target[:, :, None], axis=1), jnp.zeros((), jnp.bfloat16)).astype(jnp.bfloat16)
    grad_qkv, grad_out, grad_fc1, grad_fc2, g_bqv, g_bfc1, grad_gain, grad_vbias = totals
    return (out_slots, grad_slots, grad_qkv, grad_out, grad_fc1, grad_fc2, g_bqv.reshape(2, H, DH), g_bfc1.reshape(FF // DH, DH), grad_gain, grad_vbias)
```

```python
import math

import jax
import jax.numpy as jnp
from jax import lax
from jax.sharding import PartitionSpec as P

LN_EPS = 1e-06
HALF_ROOT = 0.7071067811865476
INV_ROOT_TAU = 0.3989422804014327
F32 = jnp.float32
BF16 = jnp.bfloat16


def norm_statistics(values):
    centered = values - jnp.mean(values, axis=-1, keepdims=True)
    variance = jnp.mean(centered * centered, axis=-1, keepdims=True)
    inverse_deviation = lax.rsqrt(variance + LN_EPS)
    return (centered * inverse_deviation, inverse_deviation)


def norm_backward(incoming, gain, unit, inverse_deviation):
    scaled = incoming * gain
    return inverse_deviation * (
        scaled
        - jnp.mean(scaled, axis=-1, keepdims=True)
        - unit * jnp.mean(scaled * unit, axis=-1, keepdims=True)
    )


def gelu_parts(pre):
    cdf = 0.5 * (1.0 + lax.erf(pre * HALF_ROOT))
    density = jnp.exp(-0.5 * pre * pre) * INV_ROOT_TAU
    return (cdf, density)


def gather_tensor(block):
    return lax.all_gather(block, "tensor", axis=0, tiled=False)


def scatter_tensor(parts):
    return lax.psum_scatter(parts, "tensor", scatter_dimension=0, tiled=False).astype(F32)


def scatter_dp(parts):
    return lax.psum_scatter(parts, "dp", scatter_dimension=0, tiled=True).astype(F32)


def dot(a, b, ca, cb):
    return lax.dot_general(a, b, (((ca,), (cb,)), ((), ())), preferred_element_type=F32)


def on_device(
    tokens, counts, w_qkv, b_qv, w_out, w_fc1, b_fc1, w_fc2, ln_gain, vec_bias, cotangent
):
    rank = lax.axis_index("tensor")
    images, cap, width = tokens.shape
    parts = counts.shape[1]
    heads, head_narrow = b_qv.shape[1], b_qv.shape[2]
    data = width // w_fc1.shape[0]
    head_dim = head_narrow * data
    cols = heads * head_dim
    hidden_cols = w_fc1.shape[1]
    narrow = width // data
    own_rows = images * cap
    rows = parts * own_rows
    scale = 1.0 / math.sqrt(head_dim)

    live = jnp.arange(cap, dtype=jnp.int32)[None, None, :] < counts.T[:, :, None]
    live_own = lax.dynamic_index_in_dim(live, rank, axis=0, keepdims=False)
    live_own = live_own.reshape(own_rows, 1)
    live_keys = live.transpose(1, 0, 2).reshape(images, 1, 1, parts * cap)

    cot_own = jnp.where(live_own, cotangent.reshape(own_rows, width), jnp.zeros((), BF16))
    tok_own = tokens.reshape(own_rows, width)

    small = jnp.concatenate(
        [
            ln_gain.reshape(-1),
            vec_bias.reshape(-1),
            b_qv.reshape(-1),
            b_fc1.reshape(-1),
        ]
    )
    small_all = lax.all_gather(small, "dp", axis=0, tiled=False)
    tok_all = gather_tensor(tok_own).reshape(rows, width)
    qkv_flat = w_qkv.transpose(1, 0, 2).reshape(narrow, 3 * cols)
    qkv_all = lax.all_gather(qkv_flat, "dp", axis=0, tiled=True)
    out_all = lax.all_gather(w_out.T, ("dp"), axis=0, tiled=True)
    out_every = gather_tensor(out_all)
    mlp_all = lax.all_gather(
        jnp.concatenate([w_fc1, w_fc2.T], axis=1), "dp", axis=0, tiled=True
    )
    cot_all = gather_tensor(cot_own).reshape(rows, width)
    fc1 = mlp_all[:, :hidden_cols]
    fc2_t = mlp_all[:, hidden_cols:]

    n0 = 2 * narrow
    n1 = n0 + 4 * narrow
    n2 = n1 + 2 * cols // data
    gain = (
        small_all[:, :n0].reshape(data, 2, narrow).transpose(1, 0, 2).reshape(2, width).astype(F32)
    )
    bias = (
        small_all[:, n0:n1].reshape(data, 4, narrow).transpose(1, 0, 2).reshape(4, width).astype(F32)
    )
    bias_qv = (
        small_all[:, n1:n2]
        .reshape(data, 2 * heads, head_narrow)
        .transpose(1, 0, 2)
        .reshape(2, cols)
        .astype(F32)
    )
    bias_hidden = (
        small_all[:, n2:]
        .reshape(data, hidden_cols // head_dim, head_narrow)
        .transpose(1, 0, 2)
        .reshape(hidden_cols)
        .astype(F32)
    )

    unit1, inv1 = norm_statistics(tok_all.astype(F32))
    a1 = (unit1 * gain[0] + bias[0]).astype(BF16)
    projected = dot(a1, qkv_all, 1, 0)

    def heads_of(flat):
        return (
            flat.reshape(parts, images, cap, heads, head_dim)
            .transpose(1, 3, 0, 2, 4)
            .reshape(images, heads, parts * cap, head_dim)
        )

    def rows_of(by_head):
        return (
            by_head.reshape(images, heads, parts, cap, head_dim)
            .transpose(2, 0, 3, 1, 4)
            .reshape(rows, cols)
        )

    queries = heads_of((projected[:, :cols] + bias_qv[0]).astype(BF16))
    keys = heads_of(projected[:, cols : 2 * cols].astype(BF16))
    values = heads_of((projected[:, 2 * cols :] + bias_qv[1]).astype(BF16))
    scores = jnp.einsum("bhqd,bhkd->bhqk", queries, keys, preferred_element_type=F32) * scale
    scores = jnp.where(live_keys, scores, -1e30)
    top = jnp.max(scores, axis=3, keepdims=True)
    log_total = top + jnp.log(jnp.sum(jnp.exp(scores - top), axis=3, keepdims=True))
    probs = jnp.exp(scores - log_total)
    probs_bf = probs.astype(BF16)
    attended = rows_of(
        jnp.einsum("bhqk,bhkd->bhqd", probs_bf, values, preferred_element_type=F32).astype(BF16)
    )
    attended_all = gather_tensor(attended)
    attn = dot(attended_all[0], out_every[0], 1, 1)
    for t in range(1, parts):
        attn = attn + dot(attended_all[t], out_every[t], 1, 1)
    resid = tok_all.astype(F32) + attn + bias[1]
    unit2, inv2 = norm_statistics(resid)
    a2 = (unit2 * gain[1] + bias[2]).astype(BF16)
    pre = dot(a2, fc1, 1, 0) + bias_hidden
    cdf, density = gelu_parts(pre)
    hidden = (pre * cdf).astype(BF16)
    d_hidden = dot(cot_all, fc2_t, 1, 0) * (cdf + pre * density)
    d_hidden_bf = d_hidden.astype(BF16)
    back2 = dot(d_hidden_bf, fc1, 1, 1)
    d_a2 = scatter_tensor(back2.astype(BF16).reshape(parts, own_rows, width))

    def own(full):
        return lax.dynamic_index_in_dim(
            full.reshape(parts, own_rows, full.shape[1]), rank, axis=0, keepdims=False
        )

    resid_own = own(resid)
    unit2_own, inv2_own = norm_statistics(resid_own)
    dy1 = jnp.where(
        live_own,
        cot_own.astype(F32) + norm_backward(d_a2, gain[1], unit2_own, inv2_own),
        0.0,
    )
    dy1_all = gather_tensor(dy1.astype(BF16)).reshape(rows, width)

    mlp_out = dot(hidden, fc2_t, 1, 1).astype(BF16)
    mlp_own = scatter_tensor(mlp_out.reshape(parts, own_rows, width))
    result = jnp.where(live_own, resid_own + mlp_own + bias[3], 0.0).astype(BF16)
    g_fc1 = dot(a2, d_hidden_bf, 0, 0)
    g_fc2 = dot(cot_all, hidden, 0, 0)
    g_mlp = scatter_dp(jnp.concatenate([g_fc1.astype(BF16), g_fc2.astype(BF16)], axis=1))

    d_att = heads_of(dot(dy1_all, out_all, 1, 0).astype(BF16))
    d_values = jnp.einsum("bhqk,bhqd->bhkd", probs_bf, d_att, preferred_element_type=F32)
    d_probs = jnp.einsum("bhqd,bhkd->bhqk", d_att, values, preferred_element_type=F32)
    delta = jnp.sum(probs * d_probs, axis=3, keepdims=True)
    d_scores = (probs * (d_probs - delta) * scale).astype(BF16)
    d_queries = jnp.einsum("bhqk,bhkd->bhqd", d_scores, keys, preferred_element_type=F32)
    d_keys = jnp.einsum("bhqk,bhqd->bhkd", d_scores, queries, preferred_element_type=F32)
    g_bqv = jnp.stack([jnp.sum(d_queries, axis=(0, 2)), jnp.sum(d_values, axis=(0, 2))])
    d_proj = jnp.concatenate(
        [rows_of(v.astype(BF16)) for v in (d_queries, d_keys, d_values)], axis=1
    )
    back1 = dot(d_proj, qkv_all, 1, 1)
    d_a1 = scatter_tensor(back1.astype(BF16).reshape(parts, own_rows, width))
    g_qkv = dot(a1, d_proj, 0, 0)
    g_out = dot(dy1_all, attended, 0, 0)
    g_att = scatter_dp(jnp.concatenate([g_qkv.astype(BF16), g_out.astype(BF16)], axis=1))

    sums = jnp.stack(
        [
            jnp.sum(back1 * unit1, axis=0),
            jnp.sum(back2 * unit2, axis=0),
            jnp.sum(back1, axis=0),
            jnp.sum(dy1, axis=0),
            jnp.sum(back2, axis=0),
            jnp.sum(cot_own.astype(F32), axis=0),
        ]
    )
    sums = lax.psum(sums, "tensor")
    lane = jnp.concatenate(
        [
            sums.reshape(6, data, narrow).transpose(1, 0, 2).reshape(data, 6 * narrow),
            g_bqv.reshape(2 * heads, data, head_narrow).transpose(1, 0, 2).reshape(data, -1),
            jnp.sum(d_hidden, axis=0)
            .reshape(hidden_cols // head_dim, data, head_narrow)
            .transpose(1, 0, 2)
            .reshape(data, -1),
        ],
        axis=1,
    )
    lane = lax.psum_scatter(lane, "dp", scatter_dimension=0, tiled=False)
    m0 = 6 * narrow
    m1 = m0 + 2 * cols // data
    sixth = lax.dynamic_index_in_dim(
        lane[:m0].reshape(6, parts, narrow // parts), rank, axis=1, keepdims=False
    )

    unit1_own, inv1_own = norm_statistics(tok_own.astype(F32))
    grad_tokens = jnp.where(
        live_own, dy1 + norm_backward(d_a1, gain[0], unit1_own, inv1_own), 0.0
    ).astype(BF16)
    return (
        result.reshape(images, cap, width),
        grad_tokens.reshape(images, cap, width),
        g_att[:, : 3 * cols].reshape(narrow, 3, cols).transpose(1, 0, 2),
        g_att[:, 3 * cols :].T,
        g_mlp[:, :hidden_cols],
        g_mlp[:, hidden_cols:].T,
        lane[m0:m1].reshape(2, heads, head_narrow),
        lane[m1:].reshape(hidden_cols // head_dim, head_narrow),
        sixth[:2],
        sixth[2:],
    )


def solution(mesh):
    in_specs = (
        P("dp", "tensor", None),
        P("dp", None),
        P(None, "dp", "tensor"),
        P(None, "tensor", "dp"),
        P("tensor", "dp"),
        P("dp", "tensor"),
        P("tensor", "dp"),
        P("tensor", "dp"),
        P(None, "dp"),
        P(None, "dp"),
        P("dp", "tensor", None),
    )
    out_specs = (
        P("dp", "tensor", None),
        P("dp", "tensor", None),
        P(None, "dp", "tensor"),
        P("tensor", "dp"),
        P("dp", "tensor"),
        P("tensor", "dp"),
        P(None, "tensor", "dp"),
        P("tensor", "dp"),
        P(None, ("dp", "tensor")),
        P(None, ("dp", "tensor")),
    )
    return jax.shard_map(
        on_device, mesh=mesh, in_specs=in_specs, out_specs=out_specs, check_vma=False
    )
```

```python
import functools
import math

import jax
import jax.numpy as jnp
from jax import lax
from jax.experimental import pallas as pl
from jax.experimental.pallas import tpu as pltpu
from jax.sharding import PartitionSpec as P

LN_EPS = 1e-06
HALF_ROOT = 0.7071067811865476
INV_ROOT_TAU = 0.3989422804014327
F32 = jnp.float32
BF16 = jnp.bfloat16


def norm_statistics(values):
    centered = values - jnp.mean(values, axis=-1, keepdims=True)
    variance = jnp.mean(centered * centered, axis=-1, keepdims=True)
    inverse_deviation = lax.rsqrt(variance + LN_EPS)
    return (centered * inverse_deviation, inverse_deviation)


def norm_backward(incoming, gain, unit, inverse_deviation):
    scaled = incoming * gain
    return inverse_deviation * (
        scaled
        - jnp.mean(scaled, axis=-1, keepdims=True)
        - unit * jnp.mean(scaled * unit, axis=-1, keepdims=True)
    )


def gelu_parts(pre):
    cdf = 0.5 * (1.0 + lax.erf(pre * HALF_ROOT))
    density = jnp.exp(-0.5 * pre * pre) * INV_ROOT_TAU
    return (cdf, density)


def exchange_kernel(plan, *refs):
    count = len(plan)
    sources = refs[:count]
    outs = refs[count : 2 * count]
    landings = refs[2 * count : -2]
    send_sems, recv_sems = refs[-2:]
    sizes = {axis: size for axis, size, _ in plan}
    barrier = pltpu.get_barrier_semaphore()
    for axis, size in sizes.items():
        me = lax.axis_index(axis)
        for step in range(1, size):
            pl.semaphore_signal(
                barrier,
                inc=1,
                device_id={axis: lax.rem(me + step, size)},
                device_id_type=pl.DeviceIdType.MESH,
            )
    pl.semaphore_wait(barrier, sum(size - 1 for size in sizes.values()))
    copies = []
    landing = 0
    for i, (axis, size, reduced) in enumerate(plan):
        me = lax.axis_index(axis)
        for step in range(1, size):
            peer = lax.rem(me + step, size)
            if reduced:
                src, dst = sources[i].at[peer], landings[landing].at[step - 1]
            else:
                src, dst = sources[i], outs[i].at[me]
            copy = pltpu.make_async_remote_copy(
                src_ref=src,
                dst_ref=dst,
                send_sem=send_sems.at[len(copies)],
                recv_sem=recv_sems.at[len(copies)],
                device_id={axis: peer},
                device_id_type=pl.DeviceIdType.MESH,
            )
            copy.start()
            copies.append(copy)
        landing += int(reduced)
    for i, (axis, size, reduced) in enumerate(plan):
        me = lax.axis_index(axis)
        if reduced:
            outs[i][...] = sources[i][me].astype(F32)
        else:
            outs[i][me] = sources[i][...]
    landing, done = 0, 0
    for i, (axis, size, reduced) in enumerate(plan):
        for step in range(1, size):
            copies[done].wait()
            done += 1
            if reduced:
                outs[i][...] += landings[landing][step - 1].astype(F32)
        landing += int(reduced)


def exchange(collective_id, *items):
    plan = tuple((axis, size, reduced) for axis, size, reduced, _ in items)
    arrays = tuple(v for _, _, _, v in items)
    out_shape = [
        jax.ShapeDtypeStruct(v.shape[1:], F32)
        if reduced
        else jax.ShapeDtypeStruct((size,) + v.shape, v.dtype)
        for _, size, reduced, v in items
    ]
    copies = sum(size - 1 for _, size, _ in plan)
    return pl.pallas_call(
        functools.partial(exchange_kernel, plan),
        out_shape=out_shape,
        in_specs=[pl.BlockSpec(memory_space=pltpu.VMEM)] * len(arrays),
        out_specs=[pl.BlockSpec(memory_space=pltpu.VMEM)] * len(arrays),
        scratch_shapes=[
            pltpu.VMEM((size - 1,) + v.shape[1:], v.dtype)
            for _, size, reduced, v in items
            if reduced
        ]
        + [pltpu.SemaphoreType.DMA((copies,)), pltpu.SemaphoreType.DMA((copies,))],
        compiler_params=pltpu.CompilerParams(
            collective_id=collective_id, has_side_effects=True
        ),
    )(*arrays)


def softmax_of(q, k, mask, scale):
    scores = dot(q, k, 1, 1) * scale + mask
    top = jnp.max(scores, axis=1, keepdims=True)
    weights = jnp.exp(scores - top)
    return weights / jnp.sum(weights, axis=1, keepdims=True)


def attention_kernel(heads, head_dim, q_ref, k_ref, v_ref, mask_ref, o_ref):
    parts, _, cap, cols = q_ref.shape
    scale = 1.0 / math.sqrt(head_dim)
    mask = mask_ref[0]
    q, k, v = (r[...].reshape(parts * cap, cols) for r in (q_ref, k_ref, v_ref))
    pieces = []
    for h in range(heads):
        c = slice(h * head_dim, (h + 1) * head_dim)
        probs = softmax_of(q[:, c], k[:, c], mask, scale).astype(BF16)
        pieces.append(dot(probs, v[:, c], 1, 0).astype(BF16))
    o_ref[...] = jnp.concatenate(pieces, axis=1).reshape(o_ref.shape)


def attention_back_kernel(
    heads, head_dim, q_ref, k_ref, v_ref, do_ref, mask_ref, d_ref, sum_ref
):
    parts, _, cap, cols = q_ref.shape
    scale = 1.0 / math.sqrt(head_dim)
    mask = mask_ref[0]
    q, k, v, d = (r[...].reshape(parts * cap, cols) for r in (q_ref, k_ref, v_ref, do_ref))
    dq, dk, dv = [], [], []
    for h in range(heads):
        c = slice(h * head_dim, (h + 1) * head_dim)
        probs = softmax_of(q[:, c], k[:, c], mask, scale)
        dv.append(dot(probs.astype(BF16), d[:, c], 0, 0))
        d_probs = dot(d[:, c], v[:, c], 1, 1)
        delta = jnp.sum(probs * d_probs, axis=1, keepdims=True)
        d_scores = (probs * (d_probs - delta) * scale).astype(BF16)
        dq.append(dot(d_scores, k[:, c], 1, 0))
        dk.append(dot(d_scores, q[:, c], 0, 0))
    dq, dk, dv = (jnp.concatenate(p, axis=1) for p in (dq, dk, dv))
    d_ref[...] = jnp.concatenate([dq, dk, dv], axis=1).astype(BF16).reshape(d_ref.shape)
    sums = jnp.concatenate(
        [jnp.sum(dq, axis=0, keepdims=True), jnp.sum(dv, axis=0, keepdims=True)], axis=0
    )

    @pl.when(pl.program_id(0) == 0)
    def _():
        sum_ref[...] = sums

    @pl.when(pl.program_id(0) > 0)
    def _():
        sum_ref[...] += sums


def image_block(v, cols):
    return pl.BlockSpec((v[0], 1, v[1], cols), lambda i: (0, i, 0, 0))


def attention(q, k, v, mask, heads):
    parts, images, cap, cols = q.shape
    block = image_block((parts, cap), cols)
    return pl.pallas_call(
        functools.partial(attention_kernel, heads, cols // heads),
        grid=(images,),
        out_shape=jax.ShapeDtypeStruct(q.shape, BF16),
        in_specs=[block] * 3 + [pl.BlockSpec((1, 1, parts * cap), lambda i: (i, 0, 0))],
        out_specs=block,
    )(q, k, v, mask)


def attention_back(q, k, v, d, mask, heads):
    parts, images, cap, cols = q.shape
    block = image_block((parts, cap), cols)
    return pl.pallas_call(
        functools.partial(attention_back_kernel, heads, cols // heads),
        grid=(images,),
        out_shape=[
            jax.ShapeDtypeStruct((parts, images, cap, 3 * cols), BF16),
            jax.ShapeDtypeStruct((2, cols), F32),
        ],
        in_specs=[block] * 4 + [pl.BlockSpec((1, 1, parts * cap), lambda i: (i, 0, 0))],
        out_specs=[
            image_block((parts, cap), 3 * cols),
            pl.BlockSpec((2, cols), lambda i: (0, 0)),
        ],
    )(q, k, v, d, mask)


def gather_tensor(block):
    return lax.all_gather(block, "tensor", axis=0, tiled=False)


def scatter_dp(parts):
    return lax.psum_scatter(parts, "dp", scatter_dimension=0, tiled=True).astype(F32)


def dot(a, b, ca, cb):
    return lax.dot_general(a, b, (((ca,), (cb,)), ((), ())), preferred_element_type=F32)


def on_device(
    tokens, counts, w_qkv, b_qv, w_out, w_fc1, b_fc1, w_fc2, ln_gain, vec_bias, cotangent
):
    rank = lax.axis_index("tensor")
    images, cap, width = tokens.shape
    parts = counts.shape[1]
    heads, head_narrow = b_qv.shape[1], b_qv.shape[2]
    data = width // w_fc1.shape[0]
    head_dim = head_narrow * data
    cols = heads * head_dim
    hidden_cols = w_fc1.shape[1]
    narrow = width // data
    own_rows = images * cap
    rows = parts * own_rows
    scale = 1.0 / math.sqrt(head_dim)

    live = jnp.arange(cap, dtype=jnp.int32)[None, None, :] < counts.T[:, :, None]
    live_own = lax.dynamic_index_in_dim(live, rank, axis=0, keepdims=False)
    live_own = live_own.reshape(own_rows, 1)
    key_mask = jnp.where(live.transpose(1, 0, 2).reshape(images, 1, parts * cap), 0.0, -1e30)

    cot_own = jnp.where(live_own, cotangent.reshape(own_rows, width), jnp.zeros((), BF16))
    tok_own = tokens.reshape(own_rows, width)

    small = jnp.concatenate(
        [
            ln_gain.reshape(-1),
            vec_bias.reshape(-1),
            b_qv.reshape(-1),
            b_fc1.reshape(-1),
        ]
    )
    lanes = 3 * cols
    pad_rows = 16 * pl.cdiv(small.size, 16 * lanes)
    small_rows = jnp.pad(small, (0, pad_rows * lanes - small.size)).reshape(pad_rows, lanes)
    qkv_flat = w_qkv.transpose(1, 0, 2).reshape(narrow, lanes)
    tok_all, out_ranks, first = exchange(
        0,
        ("tensor", parts, False, tok_own),
        ("tensor", parts, False, w_out.T),
        ("dp", data, False, jnp.concatenate([qkv_flat, small_rows], axis=0)),
    )
    tok_all = tok_all.reshape(rows, width)
    qkv_all = first[:, :narrow].reshape(width, lanes)
    small_all = first[:, narrow:].reshape(data, pad_rows * lanes)[:, : small.size]
    mlp_all = lax.all_gather(
        jnp.concatenate([w_fc1, w_fc2.T], axis=1), "dp", axis=0, tiled=True
    )
    cot_all = gather_tensor(cot_own).reshape(rows, width)
    fc1 = mlp_all[:, :hidden_cols]
    fc2_t = mlp_all[:, hidden_cols:]

    n0 = 2 * narrow
    n1 = n0 + 4 * narrow
    n2 = n1 + 2 * cols // data
    gain = (
        small_all[:, :n0].reshape(data, 2, narrow).transpose(1, 0, 2).reshape(2, width).astype(F32)
    )
    bias = (
        small_all[:, n0:n1].reshape(data, 4, narrow).transpose(1, 0, 2).reshape(4, width).astype(F32)
    )
    bias_qv = (
        small_all[:, n1:n2]
        .reshape(data, 2 * heads, head_narrow)
        .transpose(1, 0, 2)
        .reshape(2, cols)
        .astype(F32)
    )
    bias_hidden = (
        small_all[:, n2:]
        .reshape(data, hidden_cols // head_dim, head_narrow)
        .transpose(1, 0, 2)
        .reshape(hidden_cols)
        .astype(F32)
    )

    unit1, inv1 = norm_statistics(tok_all.astype(F32))
    a1 = (unit1 * gain[0] + bias[0]).astype(BF16)
    projected = dot(a1, qkv_all, 1, 0)

    shape4 = (parts, images, cap, cols)
    queries = (projected[:, :cols] + bias_qv[0]).astype(BF16).reshape(shape4)
    keys = projected[:, cols : 2 * cols].astype(BF16).reshape(shape4)
    values = (projected[:, 2 * cols :] + bias_qv[1]).astype(BF16).reshape(shape4)
    attended = attention(queries, keys, values, key_mask, heads).reshape(rows, cols)
    attended_all, out_every = exchange(
        1,
        ("tensor", parts, False, attended),
        ("dp", data, False, out_ranks.transpose(1, 0, 2).reshape(narrow, parts * cols)),
    )
    out_every = out_every.reshape(width, parts * cols)
    out_all = lax.dynamic_slice_in_dim(out_every, rank * cols, cols, axis=1)
    attended_all = attended_all.transpose(1, 0, 2).reshape(rows, parts * cols)
    attn = dot(attended_all, out_every, 1, 1)
    resid = tok_all.astype(F32) + attn + bias[1]
    unit2, inv2 = norm_statistics(resid)
    a2 = (unit2 * gain[1] + bias[2]).astype(BF16)
    pre = dot(a2, fc1, 1, 0) + bias_hidden
    cdf, density = gelu_parts(pre)
    hidden = (pre * cdf).astype(BF16)
    d_hidden = dot(cot_all, fc2_t, 1, 0) * (cdf + pre * density)
    d_hidden_bf = d_hidden.astype(BF16)
    back2 = dot(d_hidden_bf, fc1, 1, 1)
    (d_a2,) = exchange(
        2, ("tensor", parts, True, back2.astype(BF16).reshape(parts, own_rows, width))
    )

    def own(full):
        return lax.dynamic_index_in_dim(
            full.reshape(parts, own_rows, full.shape[1]), rank, axis=0, keepdims=False
        )

    resid_own = own(resid)
    unit2_own, inv2_own = norm_statistics(resid_own)
    dy1 = jnp.where(
        live_own,
        cot_own.astype(F32) + norm_backward(d_a2, gain[1], unit2_own, inv2_own),
        0.0,
    )
    (dy1_all,) = exchange(3, ("tensor", parts, False, dy1.astype(BF16)))
    dy1_all = dy1_all.reshape(rows, width)

    mlp_out = dot(hidden, fc2_t, 1, 1).astype(BF16)
    mlp_own = lax.psum_scatter(
        mlp_out.reshape(parts, own_rows, width), "tensor", scatter_dimension=0, tiled=False
    ).astype(F32)
    result = jnp.where(live_own, resid_own + mlp_own + bias[3], 0.0).astype(BF16)
    g_fc1 = dot(a2, d_hidden_bf, 0, 0)
    g_fc2 = dot(cot_all, hidden, 0, 0)
    g_mlp = scatter_dp(jnp.concatenate([g_fc1.astype(BF16), g_fc2.astype(BF16)], axis=1))

    d_att = dot(dy1_all, out_all, 1, 0).astype(BF16).reshape(shape4)
    d_proj, g_bqv = attention_back(queries, keys, values, d_att, key_mask, heads)
    d_proj = d_proj.reshape(rows, lanes)
    back1 = dot(d_proj, qkv_all, 1, 1)
    g_qkv = dot(a1, d_proj, 0, 0)
    g_out = dot(dy1_all, attended, 0, 0)
    g_att = scatter_dp(jnp.concatenate([g_qkv.astype(BF16), g_out.astype(BF16)], axis=1))

    sums = jnp.stack(
        [
            jnp.sum(back1 * unit1, axis=0),
            jnp.sum(back2 * unit2, axis=0),
            jnp.sum(back1, axis=0),
            jnp.sum(dy1, axis=0),
            jnp.sum(back2, axis=0),
            jnp.sum(cot_own.astype(F32), axis=0),
        ]
    )
    sixth_parts = (
        sums.reshape(6, data, parts, narrow // parts)
        .transpose(2, 1, 0, 3)
        .reshape(parts, data, 6 * narrow // parts)
    )
    d_a1, sixth_sums = exchange(
        4,
        ("tensor", parts, True, back1.astype(BF16).reshape(parts, own_rows, width)),
        ("tensor", parts, True, sixth_parts),
    )
    lane = jnp.concatenate(
        [
            sixth_sums,
            g_bqv.reshape(2 * heads, data, head_narrow).transpose(1, 0, 2).reshape(data, -1),
            jnp.sum(d_hidden, axis=0)
            .reshape(hidden_cols // head_dim, data, head_narrow)
            .transpose(1, 0, 2)
            .reshape(data, -1),
        ],
        axis=1,
    )
    lane_size = lane.shape[1]
    lane_rows = 8 * pl.cdiv(lane_size, 1024)
    lane = jnp.pad(lane, ((0, 0), (0, lane_rows * 128 - lane_size)))
    (lane,) = exchange(5, ("dp", data, True, lane.reshape(data, lane_rows, 128)))
    lane = lane.reshape(-1)[:lane_size]
    m0 = 6 * narrow // parts
    m1 = m0 + 2 * cols // data
    sixth = lane[:m0].reshape(6, narrow // parts)

    unit1_own, inv1_own = norm_statistics(tok_own.astype(F32))
    grad_tokens = jnp.where(
        live_own, dy1 + norm_backward(d_a1, gain[0], unit1_own, inv1_own), 0.0
    ).astype(BF16)
    return (
        result.reshape(images, cap, width),
        grad_tokens.reshape(images, cap, width),
        g_att[:, : 3 * cols].reshape(narrow, 3, cols).transpose(1, 0, 2),
        g_att[:, 3 * cols :].T,
        g_mlp[:, :hidden_cols],
        g_mlp[:, hidden_cols:].T,
        lane[m0:m1].reshape(2, heads, head_narrow),
        lane[m1:lane_size].reshape(hidden_cols // head_dim, head_narrow),
        sixth[:2],
        sixth[2:],
    )


def solution(mesh):
    in_specs = (
        P("dp", "tensor", None),
        P("dp", None),
        P(None, "dp", "tensor"),
        P(None, "tensor", "dp"),
        P("tensor", "dp"),
        P("dp", "tensor"),
        P("tensor", "dp"),
        P("tensor", "dp"),
        P(None, "dp"),
        P(None, "dp"),
        P("dp", "tensor", None),
    )
    out_specs = (
        P("dp", "tensor", None),
        P("dp", "tensor", None),
        P(None, "dp", "tensor"),
        P("tensor", "dp"),
        P("dp", "tensor"),
        P("tensor", "dp"),
        P(None, "tensor", "dp"),
        P("tensor", "dp"),
        P(None, ("dp", "tensor")),
        P(None, ("dp", "tensor")),
    )
    return jax.shard_map(
        on_device, mesh=mesh, in_specs=in_specs, out_specs=out_specs, check_vma=False
    )
```

```python
import functools
import math

import jax
import jax.numpy as jnp
from jax import lax
from jax.experimental import pallas as pl
from jax.experimental.pallas import tpu as pltpu
from jax.sharding import PartitionSpec as P

LN_EPS = 1e-06
HALF_ROOT = 0.7071067811865476
INV_ROOT_TAU = 0.3989422804014327
F32 = jnp.float32
BF16 = jnp.bfloat16


def norm_statistics(values):
    centered = values - jnp.mean(values, axis=-1, keepdims=True)
    variance = jnp.mean(centered * centered, axis=-1, keepdims=True)
    inverse_deviation = lax.rsqrt(variance + LN_EPS)
    return (centered * inverse_deviation, inverse_deviation)


def norm_backward(incoming, gain, unit, inverse_deviation):
    scaled = incoming * gain
    return inverse_deviation * (
        scaled
        - jnp.mean(scaled, axis=-1, keepdims=True)
        - unit * jnp.mean(scaled * unit, axis=-1, keepdims=True)
    )


def gelu_parts(pre):
    cdf = 0.5 * (1.0 + lax.erf(pre * HALF_ROOT))
    density = jnp.exp(-0.5 * pre * pre) * INV_ROOT_TAU
    return (cdf, density)


def exchange_kernel(plan, *refs):
    count = len(plan)
    sources = refs[:count]
    outs = refs[count : 2 * count]
    landings = refs[2 * count : -2]
    send_sems, recv_sems = refs[-2:]
    sizes = {axis: size for axis, size, _ in plan}
    barrier = pltpu.get_barrier_semaphore()
    for axis, size in sizes.items():
        me = lax.axis_index(axis)
        for step in range(1, size):
            pl.semaphore_signal(
                barrier,
                inc=1,
                device_id={axis: lax.rem(me + step, size)},
                device_id_type=pl.DeviceIdType.MESH,
            )
    pl.semaphore_wait(barrier, sum(size - 1 for size in sizes.values()))
    direct, used, landing = [], 0, 0
    chains = []
    for i, (axis, size, reduced) in enumerate(plan):
        if axis == "tensor" and not reduced:
            chains.append((i, used))
            used += 2 * (size - 1)
            continue
        me = lax.axis_index(axis)
        for step in range(1, size):
            peer = lax.rem(me + step, size)
            if reduced:
                src, dst = sources[i].at[peer], landings[landing].at[step - 1]
            else:
                src, dst = sources[i], outs[i].at[me]
            copy = pltpu.make_async_remote_copy(
                src_ref=src,
                dst_ref=dst,
                send_sem=send_sems.at[used],
                recv_sem=recv_sems.at[used],
                device_id={axis: peer},
                device_id_type=pl.DeviceIdType.MESH,
            )
            copy.start()
            direct.append((i, step, landing, copy))
            used += 1
        landing += int(reduced)

    def hop(i, first_sem, step, way):
        size = plan[i][1]
        me = lax.axis_index("tensor")
        block = lax.rem(me - way * step + size, size)
        slot = first_sem + 2 * step + (way + 1) // 2
        return pltpu.make_async_remote_copy(
            src_ref=sources[i] if step == 0 else outs[i].at[block],
            dst_ref=outs[i].at[block],
            send_sem=send_sems.at[slot],
            recv_sem=recv_sems.at[slot],
            device_id={"tensor": lax.rem(me + way + size, size)},
            device_id_type=pl.DeviceIdType.MESH,
        )

    def each_hop(step, act):
        for i, first_sem in chains:
            size = plan[i][1]
            me = lax.axis_index("tensor")
            act(i, first_sem, 1, me, size - 1 - me)
            act(i, first_sem, -1, size - 1 - me, me)

    for step in range(max([plan[i][1] - 1 for i, _ in chains], default=0)):

        def begin(i, first_sem, way, behind, ahead):
            @pl.when((behind >= step) & (ahead >= 1))
            def _():
                hop(i, first_sem, step, way).start()

        def arrive(i, first_sem, way, behind, ahead):
            @pl.when(behind >= step + 1)
            def _():
                hop(i, first_sem, step, way).wait_recv()

        each_hop(step, begin)
        if step == 0:
            for i, (axis, size, reduced) in enumerate(plan):
                if not reduced:
                    outs[i][lax.axis_index(axis)] = sources[i][...]
        each_hop(step, arrive)
    for i, (axis, size, reduced) in enumerate(plan):
        me = lax.axis_index(axis)
        if reduced:
            outs[i][...] = sources[i][me].astype(F32)
        elif not chains:
            outs[i][me] = sources[i][...]
    for i, step, landing, copy in direct:
        copy.wait()
        if plan[i][2]:
            outs[i][...] += landings[landing][step - 1].astype(F32)
    for step in range(max([plan[i][1] - 1 for i, _ in chains], default=0)):

        def end(i, first_sem, way, behind, ahead):
            @pl.when((behind >= step) & (ahead >= 1))
            def _():
                hop(i, first_sem, step, way).wait_send()

        each_hop(step, end)


def exchange(collective_id, *items):
    plan = tuple((axis, size, reduced) for axis, size, reduced, _ in items)
    arrays = tuple(v for _, _, _, v in items)
    out_shape = [
        jax.ShapeDtypeStruct(v.shape[1:], F32)
        if reduced
        else jax.ShapeDtypeStruct((size,) + v.shape, v.dtype)
        for _, size, reduced, v in items
    ]
    copies = 2 * sum(size - 1 for _, size, _ in plan)
    return pl.pallas_call(
        functools.partial(exchange_kernel, plan),
        out_shape=out_shape,
        in_specs=[pl.BlockSpec(memory_space=pltpu.VMEM)] * len(arrays),
        out_specs=[pl.BlockSpec(memory_space=pltpu.VMEM)] * len(arrays),
        scratch_shapes=[
            pltpu.VMEM((size - 1,) + v.shape[1:], v.dtype)
            for _, size, reduced, v in items
            if reduced
        ]
        + [pltpu.SemaphoreType.DMA((copies,)), pltpu.SemaphoreType.DMA((copies,))],
        compiler_params=pltpu.CompilerParams(
            collective_id=collective_id, has_side_effects=True
        ),
    )(*arrays)


def softmax_of(q, k, mask, scale):
    scores = dot(q, k, 1, 1) * scale + mask
    top = jnp.max(scores, axis=1, keepdims=True)
    weights = jnp.exp(scores - top)
    return weights / jnp.sum(weights, axis=1, keepdims=True)


def attention_kernel(heads, head_dim, q_ref, k_ref, v_ref, mask_ref, o_ref):
    parts, _, cap, cols = q_ref.shape
    scale = 1.0 / math.sqrt(head_dim)
    mask = mask_ref[0]
    q, k, v = (r[...].reshape(parts * cap, cols) for r in (q_ref, k_ref, v_ref))
    pieces = []
    for h in range(heads):
        c = slice(h * head_dim, (h + 1) * head_dim)
        probs = softmax_of(q[:, c], k[:, c], mask, scale).astype(BF16)
        pieces.append(dot(probs, v[:, c], 1, 0).astype(BF16))
    o_ref[...] = jnp.concatenate(pieces, axis=1).reshape(o_ref.shape)


def attention_back_kernel(
    heads, head_dim, q_ref, k_ref, v_ref, do_ref, mask_ref, d_ref, sum_ref
):
    parts, _, cap, cols = q_ref.shape
    scale = 1.0 / math.sqrt(head_dim)
    mask = mask_ref[0]
    q, k, v, d = (r[...].reshape(parts * cap, cols) for r in (q_ref, k_ref, v_ref, do_ref))
    dq, dk, dv = [], [], []
    for h in range(heads):
        c = slice(h * head_dim, (h + 1) * head_dim)
        probs = softmax_of(q[:, c], k[:, c], mask, scale)
        dv.append(dot(probs.astype(BF16), d[:, c], 0, 0))
        d_probs = dot(d[:, c], v[:, c], 1, 1)
        delta = jnp.sum(probs * d_probs, axis=1, keepdims=True)
        d_scores = (probs * (d_probs - delta) * scale).astype(BF16)
        dq.append(dot(d_scores, k[:, c], 1, 0))
        dk.append(dot(d_scores, q[:, c], 0, 0))
    dq, dk, dv = (jnp.concatenate(p, axis=1) for p in (dq, dk, dv))
    d_ref[...] = jnp.concatenate([dq, dk, dv], axis=1).astype(BF16).reshape(d_ref.shape)
    sums = jnp.concatenate(
        [jnp.sum(dq, axis=0, keepdims=True), jnp.sum(dv, axis=0, keepdims=True)], axis=0
    )

    @pl.when(pl.program_id(0) == 0)
    def _():
        sum_ref[...] = sums

    @pl.when(pl.program_id(0) > 0)
    def _():
        sum_ref[...] += sums


def image_block(v, cols):
    return pl.BlockSpec((v[0], 1, v[1], cols), lambda i: (0, i, 0, 0))


def attention(q, k, v, mask, heads):
    parts, images, cap, cols = q.shape
    block = image_block((parts, cap), cols)
    return pl.pallas_call(
        functools.partial(attention_kernel, heads, cols // heads),
        grid=(images,),
        out_shape=jax.ShapeDtypeStruct(q.shape, BF16),
        in_specs=[block] * 3 + [pl.BlockSpec((1, 1, parts * cap), lambda i: (i, 0, 0))],
        out_specs=block,
    )(q, k, v, mask)


def attention_back(q, k, v, d, mask, heads):
    parts, images, cap, cols = q.shape
    block = image_block((parts, cap), cols)
    return pl.pallas_call(
        functools.partial(attention_back_kernel, heads, cols // heads),
        grid=(images,),
        out_shape=[
            jax.ShapeDtypeStruct((parts, images, cap, 3 * cols), BF16),
            jax.ShapeDtypeStruct((2, cols), F32),
        ],
        in_specs=[block] * 4 + [pl.BlockSpec((1, 1, parts * cap), lambda i: (i, 0, 0))],
        out_specs=[
            image_block((parts, cap), 3 * cols),
            pl.BlockSpec((2, cols), lambda i: (0, 0)),
        ],
    )(q, k, v, d, mask)


def gather_tensor(block):
    return lax.all_gather(block, "tensor", axis=0, tiled=False)


def scatter_dp(parts):
    return lax.psum_scatter(parts, "dp", scatter_dimension=0, tiled=True).astype(F32)


def dot(a, b, ca, cb):
    return lax.dot_general(a, b, (((ca,), (cb,)), ((), ())), preferred_element_type=F32)


def on_device(
    tokens, counts, w_qkv, b_qv, w_out, w_fc1, b_fc1, w_fc2, ln_gain, vec_bias, cotangent
):
    rank = lax.axis_index("tensor")
    images, cap, width = tokens.shape
    parts = counts.shape[1]
    heads, head_narrow = b_qv.shape[1], b_qv.shape[2]
    data = width // w_fc1.shape[0]
    head_dim = head_narrow * data
    cols = heads * head_dim
    hidden_cols = w_fc1.shape[1]
    narrow = width // data
    own_rows = images * cap
    rows = parts * own_rows
    scale = 1.0 / math.sqrt(head_dim)

    live = jnp.arange(cap, dtype=jnp.int32)[None, None, :] < counts.T[:, :, None]
    live_own = lax.dynamic_index_in_dim(live, rank, axis=0, keepdims=False)
    live_own = live_own.reshape(own_rows, 1)
    key_mask = jnp.where(live.transpose(1, 0, 2).reshape(images, 1, parts * cap), 0.0, -1e30)

    cot_own = jnp.where(live_own, cotangent.reshape(own_rows, width), jnp.zeros((), BF16))
    tok_own = tokens.reshape(own_rows, width)

    small = jnp.concatenate(
        [
            ln_gain.reshape(-1),
            vec_bias.reshape(-1),
            b_qv.reshape(-1),
            b_fc1.reshape(-1),
        ]
    )
    lanes = 3 * cols
    pad_rows = 16 * pl.cdiv(small.size, 16 * lanes)
    small_rows = jnp.pad(small, (0, pad_rows * lanes - small.size)).reshape(pad_rows, lanes)
    qkv_flat = w_qkv.transpose(1, 0, 2).reshape(narrow, lanes)
    tok_all, out_ranks, first = exchange(
        0,
        ("tensor", parts, False, tok_own),
        ("tensor", parts, False, w_out.T),
        ("dp", data, False, jnp.concatenate([qkv_flat, small_rows], axis=0)),
    )
    tok_all = tok_all.reshape(rows, width)
    qkv_all = first[:, :narrow].reshape(width, lanes)
    small_all = first[:, narrow:].reshape(data, pad_rows * lanes)[:, : small.size]
    mlp_all = lax.all_gather(
        jnp.concatenate([w_fc1, w_fc2.T], axis=1), "dp", axis=0, tiled=True
    )
    cot_all = gather_tensor(cot_own).reshape(rows, width)
    fc1 = mlp_all[:, :hidden_cols]
    fc2_t = mlp_all[:, hidden_cols:]

    n0 = 2 * narrow
    n1 = n0 + 4 * narrow
    n2 = n1 + 2 * cols // data
    gain = (
        small_all[:, :n0].reshape(data, 2, narrow).transpose(1, 0, 2).reshape(2, width).astype(F32)
    )
    bias = (
        small_all[:, n0:n1].reshape(data, 4, narrow).transpose(1, 0, 2).reshape(4, width).astype(F32)
    )
    bias_qv = (
        small_all[:, n1:n2]
        .reshape(data, 2 * heads, head_narrow)
        .transpose(1, 0, 2)
        .reshape(2, cols)
        .astype(F32)
    )
    bias_hidden = (
        small_all[:, n2:]
        .reshape(data, hidden_cols // head_dim, head_narrow)
        .transpose(1, 0, 2)
        .reshape(hidden_cols)
        .astype(F32)
    )

    unit1, inv1 = norm_statistics(tok_all.astype(F32))
    a1 = (unit1 * gain[0] + bias[0]).astype(BF16)
    projected = dot(a1, qkv_all, 1, 0)

    shape4 = (parts, images, cap, cols)
    queries = (projected[:, :cols] + bias_qv[0]).astype(BF16).reshape(shape4)
    keys = projected[:, cols : 2 * cols].astype(BF16).reshape(shape4)
    values = (projected[:, 2 * cols :] + bias_qv[1]).astype(BF16).reshape(shape4)
    attended = attention(queries, keys, values, key_mask, heads).reshape(rows, cols)
    attended_all, out_every = exchange(
        1,
        ("tensor", parts, False, attended),
        ("dp", data, False, out_ranks.transpose(1, 0, 2).reshape(narrow, parts * cols)),
    )
    out_every = out_every.reshape(width, parts * cols)
    out_all = lax.dynamic_slice_in_dim(out_every, rank * cols, cols, axis=1)
    attended_all = attended_all.transpose(1, 0, 2).reshape(rows, parts * cols)
    attn = dot(attended_all, out_every, 1, 1)
    resid = tok_all.astype(F32) + attn + bias[1]
    unit2, inv2 = norm_statistics(resid)
    a2 = (unit2 * gain[1] + bias[2]).astype(BF16)
    pre = dot(a2, fc1, 1, 0) + bias_hidden
    cdf, density = gelu_parts(pre)
    hidden = (pre * cdf).astype(BF16)
    d_hidden = dot(cot_all, fc2_t, 1, 0) * (cdf + pre * density)
    d_hidden_bf = d_hidden.astype(BF16)
    back2 = dot(d_hidden_bf, fc1, 1, 1)
    (d_a2,) = exchange(
        2, ("tensor", parts, True, back2.astype(BF16).reshape(parts, own_rows, width))
    )

    def own(full):
        return lax.dynamic_index_in_dim(
            full.reshape(parts, own_rows, full.shape[1]), rank, axis=0, keepdims=False
        )

    resid_own = own(resid)
    unit2_own, inv2_own = norm_statistics(resid_own)
    dy1 = jnp.where(
        live_own,
        cot_own.astype(F32) + norm_backward(d_a2, gain[1], unit2_own, inv2_own),
        0.0,
    )
    (dy1_all,) = exchange(3, ("tensor", parts, False, dy1.astype(BF16)))
    dy1_all = dy1_all.reshape(rows, width)

    mlp_out = dot(hidden, fc2_t, 1, 1).astype(BF16)
    mlp_own = lax.psum_scatter(
        mlp_out.reshape(parts, own_rows, width), "tensor", scatter_dimension=0, tiled=False
    ).astype(F32)
    result = jnp.where(live_own, resid_own + mlp_own + bias[3], 0.0).astype(BF16)
    g_fc1 = dot(a2, d_hidden_bf, 0, 0)
    g_fc2 = dot(cot_all, hidden, 0, 0)
    g_mlp = scatter_dp(jnp.concatenate([g_fc1.astype(BF16), g_fc2.astype(BF16)], axis=1))

    d_att = dot(dy1_all, out_all, 1, 0).astype(BF16).reshape(shape4)
    d_proj, g_bqv = attention_back(queries, keys, values, d_att, key_mask, heads)
    d_proj = d_proj.reshape(rows, lanes)
    back1 = dot(d_proj, qkv_all, 1, 1)
    g_qkv = dot(a1, d_proj, 0, 0)
    g_out = dot(dy1_all, attended, 0, 0)
    g_att = scatter_dp(jnp.concatenate([g_qkv.astype(BF16), g_out.astype(BF16)], axis=1))

    sums = jnp.stack(
        [
            jnp.sum(back1 * unit1, axis=0),
            jnp.sum(back2 * unit2, axis=0),
            jnp.sum(back1, axis=0),
            jnp.sum(dy1, axis=0),
            jnp.sum(back2, axis=0),
            jnp.sum(cot_own.astype(F32), axis=0),
        ]
    )
    sixth_parts = (
        sums.reshape(6, data, parts, narrow // parts)
        .transpose(2, 1, 0, 3)
        .reshape(parts, data, 6 * narrow // parts)
    )
    d_a1, sixth_sums = exchange(
        4,
        ("tensor", parts, True, back1.astype(BF16).reshape(parts, own_rows, width)),
        ("tensor", parts, True, sixth_parts),
    )
    lane = jnp.concatenate(
        [
            sixth_sums,
            g_bqv.reshape(2 * heads, data, head_narrow).transpose(1, 0, 2).reshape(data, -1),
            jnp.sum(d_hidden, axis=0)
            .reshape(hidden_cols // head_dim, data, head_narrow)
            .transpose(1, 0, 2)
            .reshape(data, -1),
        ],
        axis=1,
    )
    lane_size = lane.shape[1]
    lane_rows = 8 * pl.cdiv(lane_size, 1024)
    lane = jnp.pad(lane, ((0, 0), (0, lane_rows * 128 - lane_size)))
    (lane,) = exchange(5, ("dp", data, True, lane.reshape(data, lane_rows, 128)))
    lane = lane.reshape(-1)[:lane_size]
    m0 = 6 * narrow // parts
    m1 = m0 + 2 * cols // data
    sixth = lane[:m0].reshape(6, narrow // parts)

    unit1_own, inv1_own = norm_statistics(tok_own.astype(F32))
    grad_tokens = jnp.where(
        live_own, dy1 + norm_backward(d_a1, gain[0], unit1_own, inv1_own), 0.0
    ).astype(BF16)
    return (
        result.reshape(images, cap, width),
        grad_tokens.reshape(images, cap, width),
        g_att[:, : 3 * cols].reshape(narrow, 3, cols).transpose(1, 0, 2),
        g_att[:, 3 * cols :].T,
        g_mlp[:, :hidden_cols],
        g_mlp[:, hidden_cols:].T,
        lane[m0:m1].reshape(2, heads, head_narrow),
        lane[m1:lane_size].reshape(hidden_cols // head_dim, head_narrow),
        sixth[:2],
        sixth[2:],
    )


def solution(mesh):
    in_specs = (
        P("dp", "tensor", None),
        P("dp", None),
        P(None, "dp", "tensor"),
        P(None, "tensor", "dp"),
        P("tensor", "dp"),
        P("dp", "tensor"),
        P("tensor", "dp"),
        P("tensor", "dp"),
        P(None, "dp"),
        P(None, "dp"),
        P("dp", "tensor", None),
    )
    out_specs = (
        P("dp", "tensor", None),
        P("dp", "tensor", None),
        P(None, "dp", "tensor"),
        P("tensor", "dp"),
        P("dp", "tensor"),
        P("tensor", "dp"),
        P(None, "tensor", "dp"),
        P("tensor", "dp"),
        P(None, ("dp", "tensor")),
        P(None, ("dp", "tensor")),
    )
    return jax.shard_map(
        on_device, mesh=mesh, in_specs=in_specs, out_specs=out_specs, check_vma=False
    )
```
